32 devices in a mesh: img: 8 (over y, x, core), own: 4 (over z).
Axes of the slice: x: 2, y: 2, z: 4, core: 2. Of those that a mesh axis runs over, the one named last changes fastest.
Arguments:
- patches: bfloat16 [6272, 4608], P(('img', 'own')), may hold values from -6 to 6
- grads: bfloat16 [6272, 512], P(('img', 'own')), may hold values from -0.8984375 to 0.8984375
- basis_g: bfloat16 [512, 512], replicated, may hold values from -0.25 to 0.25
- basis_slots: bfloat16 [4608, 9216], P(None, 'own'), may hold values from -0.09375 to 0.09375
- col_counts: int32 [4], replicated, may hold values from 1 to 2304, 4608 in all
Outputs:
- corrections: float32 [4608, 512], P(('img', 'own'))
The draws below stay inside these ranges and needn't reach their ends.
Inputs may be any that keep to these rules, and one draw needn't show every extreme that they name: `col_counts`: the counts sum to 4608; one owner has exactly 2304.
All inputs are finite; a program needn't handle non-finite values.
Results may differ from the reference program's by a relative error of at most 0.00049.
Values may be sent and summed in bfloat16 or wider, within the bound.
A program may use at most 128 MiB of HBM per device.

```python
import math
import jax
import jax.numpy as jnp
import numpy as np
from jax import lax

KIN = 4608
GOUT = 512
POS = 49
IMG_DEV = 4
CAP = 2304
IMAGES = 128
ROWS = 6272
N_OWN = 4


def levels(key, dims, split, smallest, top_value):
    level = 1.0
    for position, shards_of in split:
        heights = jax.random.uniform(jax.random.fold_in(jax.random.fold_in(key, 6), position), (shards_of,), jnp.float32, smallest / len(split), top_value / len(split))
        level = level * jnp.repeat(jnp.exp(heights), dims[position] // shards_of).reshape((-1,) + (1,) * (len(dims) - 1 - position))
    return level


def length_profile(number_of, total, limit, lean):
    weights = [(1 << 20) // math.isqrt(rank ** lean) + 1 for rank in range(2, number_of + 1)]
    surplus, given = total - limit - (number_of - 1), [1] * (number_of - 1)
    while surplus > 0:
        free = [i for i in range(number_of - 1) if given[i] < limit]
        pool, left = sum([weights[i] for i in free]), surplus
        for i in free:
            extra = min(limit - given[i], max(1, left * weights[i] // pool), surplus)
            given[i] = given[i] + extra
            surplus = surplus - extra
    return np.array([limit] + given)


def ragged_sizes(key, count, total, bound, skew):
    if count == 2:
        one = jax.random.randint(key, (), max(1, total - bound), min(bound, total - 1) + 1)
        return jnp.stack([one, total - one])
    lengths = jnp.asarray(length_profile(count, total, bound, skew), jnp.int32)
    pairs = (count - 1) // 2
    giver, receiver = lengths[1:1 + 2 * pairs:2], lengths[2:2 + 2 * pairs:2]
    room = jnp.minimum(giver - 1, bound - receiver)
    passed = jax.random.randint(jax.random.fold_in(key, 1), (pairs,), 0, 1 << 20) % (room + 1)
    lengths = lengths.at[1:1 + 2 * pairs:2].set(giver - passed).at[2:2 + 2 * pairs:2].set(receiver + passed)
    return lengths[jax.random.permutation(jax.random.fold_in(key, 2), count)]


def gaussian(stream_key, dims, width, limit, split=(), held_as=jnp.bfloat16):
    entries = width * jax.random.normal(stream_key, dims, jnp.float32)
    if split:
        entries = entries * levels(stream_key, dims, split, -0.22, 0.18)
    return jnp.clip(entries, -limit, limit).astype(held_as)


def setup_inputs(seed: int = 0) -> dict:
    seeds = jax.random.split(jax.random.key(seed), 6)
    return {
        "patches": gaussian(seeds[0], (ROWS, KIN), 1.0, 6.0, ((0, 32),)),
        "grads": gaussian(seeds[1], (ROWS, GOUT), 0.15, 0.8984375, ((0, 32),)),
        "basis_g": gaussian(seeds[2], (GOUT, GOUT), GOUT ** -0.5, 0.25),
        "basis_slots": gaussian(seeds[3], (KIN, N_OWN * CAP), KIN ** -0.5, 0.09375, ((1, 4),)),
        "col_counts": ragged_sizes(seeds[4], N_OWN, KIN, CAP, 2).astype(jnp.int32),
    }


def reference(patches, grads, basis_g, basis_slots, col_counts):
    block = IMG_DEV
    steps_count = IMAGES // block
    patch_blocks = patches.reshape(steps_count, block * POS, KIN)
    grad_blocks = grads.reshape(steps_count, block * POS, GOUT)

    def accumulate(total, pieces):
        patch_piece, grad_piece = pieces
        proj_g = jnp.dot(grad_piece, basis_g, preferred_element_type=jnp.float32).astype(jnp.bfloat16)
        proj_a = jnp.dot(patch_piece, basis_slots, preferred_element_type=jnp.float32).astype(jnp.bfloat16)
        proj_g = proj_g.reshape(block, POS, GOUT).astype(jnp.float32)
        proj_a = proj_a.reshape(block, POS, N_OWN * CAP).astype(jnp.float32)
        coef = jnp.einsum("nps,npg->nsg", proj_a, proj_g)
        return total + jnp.sum(coef * coef, axis=0), None

    start_total = jnp.zeros((N_OWN * CAP, GOUT), jnp.float32)
    slot_corr, unused = lax.scan(accumulate, start_total, (patch_blocks, grad_blocks))
    slot_corr = slot_corr / jnp.float32(IMAGES)
    counts = col_counts.astype(jnp.int32)
    starts = (jnp.cumsum(counts) - counts).astype(jnp.int32)
    slot_index = jnp.arange(CAP, dtype=jnp.int32)
    result = jnp.zeros((KIN + CAP, GOUT), jnp.float32)
    for owner in range(N_OWN):
        piece = slot_corr[owner * CAP:(owner + 1) * CAP]
        piece = jnp.where((slot_index < counts[owner])[:, None], piece, jnp.float32(0.0))
        placed = lax.dynamic_update_slice(jnp.zeros((KIN + CAP, GOUT), jnp.float32), piece, (starts[owner], jnp.int32(0)))
        result = result + placed
    return result[:KIN]
```

```python
import functools

import jax
import jax.numpy as jnp
from jax import lax
from jax.experimental import pallas as pl
from jax.experimental.pallas import tpu as pltpu
from jax.sharding import PartitionSpec as P

POS = 49
PIECE = 768
MESH = pl.DeviceIdType.MESH


def widest(total, most):
    return max(w for w in range(128, most + 1, 128) if total % w == 0)


def project(n, images, x_hbm, g_hbm, bg_ref, b_hbm, corr, xbuf, gbuf, bbuf, acc, proj, masked,
            x_sem, g_sem, b_sem, recv, g_recv, right_sem, left_sem, g_right, g_left):
    me = lax.axis_index("own")
    pieces, width, slots = bbuf.shape
    rows = x_hbm.shape[0]
    gout = bg_ref.shape[1]
    tile = widest(slots, 768)
    strip = widest(slots, 256)
    has_left, has_right = me > 0, me < n - 1

    def own_piece(q):
        return pltpu.make_async_copy(
            x_hbm.at[:, pl.ds(pl.multiple_of(q * width, width), width)], xbuf.at[me, q], x_sem.at[q])

    def basis_piece(q):
        return pltpu.make_async_copy(
            b_hbm.at[pl.ds(pl.multiple_of(q * width, width), width)], bbuf.at[q], b_sem.at[q])

    own_g = pltpu.make_async_copy(g_hbm, gbuf.at[me], g_sem)

    def send(chunk, q, to, sem):
        return pltpu.make_async_remote_copy(
            xbuf.at[chunk, q], xbuf.at[chunk, q], sem.at[chunk, q], recv.at[chunk, q],
            device_id={"own": to}, device_id_type=MESH)

    def send_g(chunk, to, sem):
        return pltpu.make_async_remote_copy(
            gbuf.at[chunk], gbuf.at[chunk], sem.at[chunk], g_recv.at[chunk],
            device_id={"own": to}, device_id_type=MESH)

    own_g.start()
    for q in range(pieces):
        own_piece(q).start()
    for q in range(pieces):
        basis_piece(q).start()

    barrier = pltpu.get_barrier_semaphore()

    @pl.when(has_left)
    def _():
        pl.semaphore_signal(barrier, inc=1, device_id={"own": me - 1}, device_id_type=MESH)

    @pl.when(has_right)
    def _():
        pl.semaphore_signal(barrier, inc=1, device_id={"own": me + 1}, device_id_type=MESH)

    pl.semaphore_wait(barrier, has_left.astype(jnp.int32) + has_right.astype(jnp.int32))

    own_g.wait()

    @pl.when(has_right)
    def _():
        send_g(me, me + 1, g_right).start()

    @pl.when(has_left)
    def _():
        send_g(me, me - 1, g_left).start()

    def send_own(q, carry):
        own_piece(q).wait()

        @pl.when(has_right)
        def _():
            send(me, q, me + 1, right_sem).start()

        @pl.when(has_left)
        def _():
            send(me, q, me - 1, left_sem).start()
        return carry

    lax.fori_loop(0, pieces, send_own, 0)

    acc[...] = jnp.zeros_like(acc)
    proj[...] = jnp.zeros_like(proj)
    corr[...] = jnp.zeros_like(corr)

    def multiply(chunk, q, side):
        def one(t, carry):
            columns = pl.ds(pl.multiple_of(t * tile, tile), tile)
            acc[side, pl.ds(0, rows), columns] += jnp.dot(
                xbuf[chunk, q], bbuf[q, :, columns], preferred_element_type=jnp.float32)
            return carry
        lax.fori_loop(0, slots // tile, one, 0)

    def finish(chunk, side):
        proj[pl.ds(0, rows), :] = jnp.dot(gbuf[chunk], bg_ref[...], preferred_element_type=jnp.float32)
        whole = proj[...]
        row = lax.broadcasted_iota(jnp.int32, whole.shape, 0)
        for image in range(images):
            inside = (row >= image * POS) & (row < (image + 1) * POS)
            masked[:, image * gout:(image + 1) * gout] = jnp.where(inside, whole, 0.0).astype(jnp.bfloat16)

        def one(t, carry):
            columns = pl.ds(pl.multiple_of(t * strip, strip), strip)
            coef = lax.dot_general(
                acc[side, :, columns].astype(jnp.bfloat16), masked[...], (((0,), (0,)), ((), ())),
                preferred_element_type=jnp.float32)
            total = corr[columns, :]
            for image in range(images):
                part = coef[:, image * gout:(image + 1) * gout]
                total = total + part * part
            corr[columns, :] = total
            acc[side, :, columns] = jnp.zeros((acc.shape[1], strip), jnp.float32)
            return carry
        lax.fori_loop(0, slots // strip, one, 0)

    def at_distance(d, carry):
        def chunk_of(side):
            return me - d + 2 * d * side

        def present(side):
            chunk = chunk_of(side)
            return (chunk >= 0) & (chunk < n) & ((d > 0) | (side == 0))

        def on_piece(q, carry):
            def on_side(side, carry):
                chunk = chunk_of(side)

                @pl.when(present(side))
                def _():
                    @pl.when(d == 0)
                    def _():
                        basis_piece(q).wait()

                    @pl.when(d > 0)
                    def _():
                        send(chunk, q, me, right_sem).wait_recv()

                        @pl.when((side == 0) & has_right)
                        def _():
                            send(chunk, q, me + 1, right_sem).start()

                        @pl.when((side == 1) & has_left)
                        def _():
                            send(chunk, q, me - 1, left_sem).start()
                    multiply(chunk, q, side)
                return carry
            return lax.fori_loop(0, 2, on_side, carry)
        lax.fori_loop(0, pieces, on_piece, 0)

        def on_end(side, carry):
            chunk = chunk_of(side)

            @pl.when(present(side))
            def _():
                finish(chunk, side)
            return carry

        def on_grads(side, carry):
            chunk = chunk_of(side)

            @pl.when(present(side) & (d > 0))
            def _():
                send_g(chunk, me, g_right).wait_recv()

                @pl.when((side == 0) & has_right)
                def _():
                    send_g(chunk, me + 1, g_right).start()

                @pl.when((side == 1) & has_left)
                def _():
                    send_g(chunk, me - 1, g_left).start()
            return carry
        lax.fori_loop(0, 2, on_grads, 0)
        lax.fori_loop(0, 2, on_end, 0)
        return carry

    lax.fori_loop(0, n, at_distance, 0)

    def drain(chunk, carry):
        @pl.when((chunk <= me) & has_right)
        def _():
            send_g(chunk, me + 1, g_right).wait_send()

        @pl.when((chunk >= me) & has_left)
        def _():
            send_g(chunk, me - 1, g_left).wait_send()

        def one(q, carry):
            @pl.when((chunk <= me) & has_right)
            def _():
                send(chunk, q, me + 1, right_sem).wait_send()

            @pl.when((chunk >= me) & has_left)
            def _():
                send(chunk, q, me - 1, left_sem).wait_send()
            return carry
        lax.fori_loop(0, pieces, one, 0)
        return carry

    lax.fori_loop(0, n, drain, 0)


def partial_corr(n, patches, grads, basis_g, basis_slots):
    rows, kin = patches.shape
    gout = basis_g.shape[1]
    slots = basis_slots.shape[1]
    width = widest(kin, PIECE)
    pieces = kin // width
    padded = -(-rows // 256) * 256
    images = rows // POS
    dma = pltpu.SemaphoreType.DMA
    return pl.pallas_call(
        functools.partial(project, n, images),
        out_shape=jax.ShapeDtypeStruct((slots, gout), jnp.float32),
        in_specs=[
            pl.BlockSpec(memory_space=pl.ANY),
            pl.BlockSpec(memory_space=pl.ANY),
            pl.BlockSpec(memory_space=pltpu.VMEM),
            pl.BlockSpec(memory_space=pl.ANY),
        ],
        out_specs=pl.BlockSpec(memory_space=pltpu.VMEM),
        scratch_shapes=[
            pltpu.VMEM((n, pieces, rows, width), jnp.bfloat16),
            pltpu.VMEM((n, rows, gout), jnp.bfloat16),
            pltpu.VMEM((pieces, width, slots), jnp.bfloat16),
            pltpu.VMEM((2, padded, slots), jnp.float32),
            pltpu.VMEM((padded, gout), jnp.float32),
            pltpu.VMEM((padded, images * gout), jnp.bfloat16),
            dma((pieces,)), dma, dma((pieces,)),
            dma((n, pieces)), dma((n,)), dma((n, pieces)), dma((n, pieces)), dma((n,)), dma((n,)),
        ],
        compiler_params=pltpu.CompilerParams(
            collective_id=0, has_side_effects=True, vmem_limit_bytes=60 * 1024 * 1024),
    )(patches, grads, basis_g, basis_slots)


def shards(patches, grads, basis_g, basis_slots, col_counts):
    groups = lax.axis_size("img")
    owners = lax.axis_size("own")
    owner_id = lax.axis_index("own")
    kin, slots = basis_slots.shape
    gout = basis_g.shape[1]
    total_images = patches.shape[0] // POS * groups * owners
    corr = partial_corr(owners, patches, grads, basis_g, basis_slots)
    starts = jnp.cumsum(col_counts) - col_counts
    my_count = lax.dynamic_index_in_dim(col_counts, owner_id, keepdims=False)
    my_start = lax.dynamic_index_in_dim(starts, owner_id, keepdims=False)
    shift = lax.rem(my_start, jnp.int32(slots))
    rolled = lax.dynamic_slice_in_dim(jnp.concatenate([corr, corr], axis=0), slots - shift, slots, 0)
    kept = lax.psum_scatter(rolled, "img", scatter_dimension=0, tiled=True) / jnp.float32(total_images)
    held = slots // groups
    wraps = kin // slots
    block = kin // (groups * owners)
    subs = held // block
    position = lax.axis_index("img") * held + jnp.arange(held, dtype=jnp.int32)
    final = position[None, :] + jnp.arange(wraps, dtype=jnp.int32)[:, None] * slots
    valid = (final >= my_start) & (final < my_start + my_count)
    laid = jnp.where(valid[:, :, None], kept[None], jnp.float32(0.0)).reshape(owners * block, gout)
    mine = lax.psum_scatter(laid, "own", scatter_dimension=0, tiled=True)
    moves = []
    for j in range(groups):
        for o in range(owners):
            moves.append((j * owners + o, (o // subs) * (slots // block) + j * subs + o % subs))
    return lax.ppermute(mine, ("img", "own"), moves)


def solution(mesh):
    in_specs = (P(("img", "own"), None), P(("img", "own"), None), P(), P(None, "own"), P())
    out_specs = P(("img", "own"), None)
    return jax.shard_map(shards, mesh=mesh, in_specs=in_specs, out_specs=out_specs, check_vma=False)
```

```python
import functools

import jax
import jax.numpy as jnp
from jax import lax
from jax.experimental import pallas as pl
from jax.experimental.pallas import tpu as pltpu
from jax.sharding import PartitionSpec as P

POS = 49
PIECE = 768
MESH = pl.DeviceIdType.MESH


def widest(total, most):
    return max(w for w in range(128, most + 1, 128) if total % w == 0)


def project(n, images, x_hbm, g_hbm, bg_ref, b_hbm, corr, xbuf, gbuf, bbuf, acc, proj, masked,
            x_sem, g_sem, b_sem, recv, g_recv, right_sem, left_sem, g_right, g_left):
    me = lax.axis_index("own")
    pieces, width, slots = bbuf.shape
    rows = x_hbm.shape[0]
    gout = bg_ref.shape[1]
    tile = widest(slots, 768)
    strip = widest(slots, 256)
    has_left, has_right = me > 0, me < n - 1

    def own_piece(q):
        return pltpu.make_async_copy(
            x_hbm.at[:, pl.ds(pl.multiple_of(q * width, width), width)], xbuf.at[me, q], x_sem.at[q])

    def basis_piece(q):
        return pltpu.make_async_copy(
            b_hbm.at[pl.ds(pl.multiple_of(q * width, width), width)], bbuf.at[q], b_sem.at[q])

    own_g = pltpu.make_async_copy(g_hbm, gbuf.at[me], g_sem)

    def send(chunk, q, to, sem):
        return pltpu.make_async_remote_copy(
            xbuf.at[chunk, q], xbuf.at[chunk, q], sem.at[chunk, q], recv.at[chunk, q],
            device_id={"own": to}, device_id_type=MESH)

    def send_g(chunk, to, sem):
        return pltpu.make_async_remote_copy(
            gbuf.at[chunk], gbuf.at[chunk], sem.at[chunk], g_recv.at[chunk],
            device_id={"own": to}, device_id_type=MESH)

    own_g.start()
    for q in range(pieces):
        own_piece(q).start()
    for q in range(pieces):
        basis_piece(q).start()

    barrier = pltpu.get_barrier_semaphore()

    @pl.when(has_left)
    def _():
        pl.semaphore_signal(barrier, inc=1, device_id={"own": me - 1}, device_id_type=MESH)

    @pl.when(has_right)
    def _():
        pl.semaphore_signal(barrier, inc=1, device_id={"own": me + 1}, device_id_type=MESH)

    pl.semaphore_wait(barrier, has_left.astype(jnp.int32) + has_right.astype(jnp.int32))

    own_g.wait()

    @pl.when(has_right)
    def _():
        send_g(me, me + 1, g_right).start()

    @pl.when(has_left)
    def _():
        send_g(me, me - 1, g_left).start()

    def send_own(q, carry):
        own_piece(q).wait()

        @pl.when(has_right)
        def _():
            send(me, q, me + 1, right_sem).start()

        @pl.when(has_left)
        def _():
            send(me, q, me - 1, left_sem).start()
        return carry

    lax.fori_loop(0, pieces, send_own, 0)

    acc[...] = jnp.zeros_like(acc)
    proj[...] = jnp.zeros_like(proj)
    corr[...] = jnp.zeros_like(corr)

    def multiply(chunk, q, side):
        def one(t, carry):
            columns = pl.ds(pl.multiple_of(t * tile, tile), tile)
            acc[side, pl.ds(0, rows), columns] += jnp.dot(
                xbuf[chunk, q], bbuf[q, :, columns], preferred_element_type=jnp.float32)
            return carry
        lax.fori_loop(0, slots // tile, one, 0)

    def finish(chunk, side):
        proj[pl.ds(0, rows), :] = jnp.dot(gbuf[chunk], bg_ref[...], preferred_element_type=jnp.float32)
        whole = proj[...]
        row = lax.broadcasted_iota(jnp.int32, whole.shape, 0)
        for image in range(images):
            inside = (row >= image * POS) & (row < (image + 1) * POS)
            masked[:, image * gout:(image + 1) * gout] = jnp.where(inside, whole, 0.0).astype(jnp.bfloat16)

        def one(t, carry):
            columns = pl.ds(pl.multiple_of(t * strip, strip), strip)
            coef = lax.dot_general(
                acc[side, :, columns].astype(jnp.bfloat16), masked[...], (((0,), (0,)), ((), ())),
                preferred_element_type=jnp.float32)
            total = corr[columns, :]
            for image in range(images):
                part = coef[:, image * gout:(image + 1) * gout]
                total = total + part * part
            corr[columns, :] = total
            acc[side, :, columns] = jnp.zeros((acc.shape[1], strip), jnp.float32)
            return carry
        lax.fori_loop(0, slots // strip, one, 0)

    def at_distance(d, carry):
        def chunk_of(side):
            return me - d + 2 * d * side

        def present(side):
            chunk = chunk_of(side)
            return (chunk >= 0) & (chunk < n) & ((d > 0) | (side == 0))

        def on_piece(q, carry):
            def on_side(side, carry):
                chunk = chunk_of(side)

                @pl.when(present(side))
                def _():
                    @pl.when(d == 0)
                    def _():
                        basis_piece(q).wait()

                    @pl.when(d > 0)
                    def _():
                        send(chunk, q, me, right_sem).wait_recv()

                        @pl.when((side == 0) & has_right)
                        def _():
                            send(chunk, q, me + 1, right_sem).start()

                        @pl.when((side == 1) & has_left)
                        def _():
                            send(chunk, q, me - 1, left_sem).start()
                    multiply(chunk, q, side)
                return carry
            return lax.fori_loop(0, 2, on_side, carry)
        lax.fori_loop(0, pieces, on_piece, 0)

        def on_end(side, carry):
            chunk = chunk_of(side)

            @pl.when(present(side))
            def _():
                finish(chunk, side)
            return carry

        def on_grads(side, carry):
            chunk = chunk_of(side)

            @pl.when(present(side) & (d > 0))
            def _():
                send_g(chunk, me, g_right).wait_recv()

                @pl.when((side == 0) & has_right)
                def _():
                    send_g(chunk, me + 1, g_right).start()

                @pl.when((side == 1) & has_left)
                def _():
                    send_g(chunk, me - 1, g_left).start()
            return carry
        lax.fori_loop(0, 2, on_grads, 0)
        lax.fori_loop(0, 2, on_end, 0)
        return carry

    lax.fori_loop(0, n, at_distance, 0)

    def drain(chunk, carry):
        @pl.when((chunk <= me) & has_right)
        def _():
            send_g(chunk, me + 1, g_right).wait_send()

        @pl.when((chunk >= me) & has_left)
        def _():
            send_g(chunk, me - 1, g_left).wait_send()

        def one(q, carry):
            @pl.when((chunk <= me) & has_right)
            def _():
                send(chunk, q, me + 1, right_sem).wait_send()

            @pl.when((chunk >= me) & has_left)
            def _():
                send(chunk, q, me - 1, left_sem).wait_send()
            return carry
        lax.fori_loop(0, pieces, one, 0)
        return carry

    lax.fori_loop(0, n, drain, 0)


def partial_corr(n, patches, grads, basis_g, basis_slots):
    rows, kin = patches.shape
    gout = basis_g.shape[1]
    slots = basis_slots.shape[1]
    width = widest(kin, PIECE)
    pieces = kin // width
    padded = -(-rows // 256) * 256
    images = rows // POS
    dma = pltpu.SemaphoreType.DMA
    return pl.pallas_call(
        functools.partial(project, n, images),
        out_shape=jax.ShapeDtypeStruct((slots, gout), jnp.float32),
        in_specs=[
            pl.BlockSpec(memory_space=pl.ANY),
            pl.BlockSpec(memory_space=pl.ANY),
            pl.BlockSpec(memory_space=pltpu.VMEM),
            pl.BlockSpec(memory_space=pl.ANY),
        ],
        out_specs=pl.BlockSpec(memory_space=pltpu.VMEM),
        scratch_shapes=[
            pltpu.VMEM((n, pieces, rows, width), jnp.bfloat16),
            pltpu.VMEM((n, rows, gout), jnp.bfloat16),
            pltpu.VMEM((pieces, width, slots), jnp.bfloat16),
            pltpu.VMEM((2, padded, slots), jnp.float32),
            pltpu.VMEM((padded, gout), jnp.float32),
            pltpu.VMEM((padded, images * gout), jnp.bfloat16),
            dma((pieces,)), dma, dma((pieces,)),
            dma((n, pieces)), dma((n,)), dma((n, pieces)), dma((n, pieces)), dma((n,)), dma((n,)),
        ],
        compiler_params=pltpu.CompilerParams(
            collective_id=0, has_side_effects=True, vmem_limit_bytes=60 * 1024 * 1024),
    )(patches, grads, basis_g, basis_slots)


def spread(n, groups, wraps, halves, total_images, counts, x_ref, out_ref, *scratch):
    bits = groups.bit_length() - 1
    recv, sums = scratch[:bits], scratch[bits:2 * bits]
    send_sem, recv_sem = scratch[2 * bits:3 * bits], scratch[3 * bits:4 * bits]
    collected, final, landed, z_send, z_recv, y_send, y_recv = scratch[4 * bits:]
    j, o = lax.axis_index("img"), lax.axis_index("own")
    blocks, rows, gout = x_ref.shape
    part = gout // halves
    run = groups // wraps
    streams = blocks // groups
    level = j // run
    bit = [(j // 2 ** b) % 2 for b in range(bits)]
    orders = [[0] + list(range(1, bits)), [0] + list(range(bits - 1, 0, -1))]

    def partner(b):
        return j + 2 ** b - 2 ** (b + 1) * bit[b]

    def cols(h):
        return pl.ds(h * part, part)

    barrier = pltpu.get_barrier_semaphore()
    greeted = 0
    for b in range(bits):
        pl.semaphore_signal(barrier, inc=1, device_id={"img": partner(b)}, device_id_type=MESH)
        greeted += 1
    for step in range(1, n):
        pl.semaphore_signal(barrier, inc=1, device_id={"own": lax.rem(o + step, n)}, device_id_type=MESH)
        greeted += 1
    for step in range(1, wraps):
        pl.semaphore_signal(barrier, inc=1, device_id={"img": lax.rem(j + step * run, groups)}, device_id_type=MESH)
        greeted += 1
    pl.semaphore_wait(barrier, greeted)

    def block_of(owner, stream):
        return n * (owner % run) + (owner // run + owner) % wraps + wraps * stream

    def source(stream, t, e, flip):
        order = orders[stream]
        if t == 0:
            owner = 0
            for i, b in enumerate(order):
                if i == 0:
                    value = 1 - bit[b] if flip else bit[b]
                else:
                    value = (e >> (i - 1)) & 1
                owner = owner + value * 2 ** b
            return x_ref.at[block_of(owner, stream)]
        value = 1 - bit[order[t]] if flip else bit[order[t]]
        return sums[t - 1].at[stream, value + 2 * e]

    def exchange(stream, t, e, h):
        return pltpu.make_async_remote_copy(
            source(stream, t, e, True).at[:, cols(h)], recv[t].at[stream, e, :, cols(h)],
            send_sem[t].at[stream, e, h], recv_sem[t].at[stream, e, h],
            device_id={"img": partner(orders[stream][t])}, device_id_type=MESH)

    def fan(t):
        return groups >> (t + 1)

    for h in range(halves):
        for stream in range(streams):
            for e in range(fan(0)):
                exchange(stream, 0, e, h).start()

    collects = [o == (level + j) % wraps + wraps * stream for stream in range(streams)]
    collector = collects[0]
    for other in collects[1:]:
        collector = collector | other

    def to_collector(stream, h):
        return pltpu.make_async_remote_copy(
            sums[bits - 1].at[stream, 0, :, cols(h)], collected.at[o, :, cols(h)],
            z_send.at[stream, h], z_recv.at[o, h],
            device_id={"own": (level + j) % wraps + wraps * stream}, device_id_type=MESH)

    for t in range(bits):
        for h in range(halves):
            for stream in range(streams):
                for e in range(fan(t)):
                    exchange(stream, t, e, h).wait_recv()
                    sums[t][stream, e, :, cols(h)] = (
                        source(stream, t, e, False)[:, cols(h)] + recv[t][stream, e, :, cols(h)])
                if t + 1 < bits:
                    for e in range(fan(t + 1)):
                        exchange(stream, t + 1, e, h).start()
                else:
                    @pl.when(collects[stream])
                    def _():
                        collected[o, :, cols(h)] = sums[t][stream, 0, :, cols(h)]

                    @pl.when(jnp.logical_not(collects[stream]))
                    def _():
                        to_collector(stream, h).start()

    def onward(wrap, h):
        return pltpu.make_async_remote_copy(
            final.at[wrap, :, cols(h)], landed.at[:, cols(h)], y_send.at[wrap, h], y_recv.at[h],
            device_id={"img": j % run + run * wrap}, device_id_type=MESH)

    first, begins = jnp.int32(0), []
    for owner in range(n):
        begins.append(first)
        first = first + counts[owner]

    for h in range(halves):
        @pl.when(collector)
        def _():
            for step in range(1, n):
                who = lax.rem(o + step, n)
                pltpu.make_async_remote_copy(
                    collected.at[who, :, cols(h)], collected.at[who, :, cols(h)],
                    z_send.at[0, h], z_recv.at[who, h],
                    device_id={"own": who}, device_id_type=MESH).wait_recv()
            for wrap in range(wraps):
                row = (wrap * blocks + n * (j % run) + o) * rows + lax.broadcasted_iota(
                    jnp.int32, (rows, part), 0)
                value = jnp.zeros((rows, part), jnp.float32)
                for owner in range(n):
                    mine = (row >= begins[owner]) & (row < begins[owner] + counts[owner])
                    value = jnp.where(mine, collected[owner, :, cols(h)], value)
                final[wrap, :, cols(h)] = value / jnp.float32(total_images)

                @pl.when(level != wrap)
                def _():
                    onward(wrap, h).start()

                @pl.when(level == wrap)
                def _():
                    out_ref[:, cols(h)] = final[wrap, :, cols(h)]

    from_self = lax.rem(o - j + wraps * (groups + 1), wraps) == level
    for h in range(halves):
        @pl.when(jnp.logical_not(from_self))
        def _():
            onward(0, h).wait_recv()
            out_ref[:, cols(h)] = landed[:, cols(h)]

    for h in range(halves):
        for stream in range(streams):
            for t in range(bits):
                for e in range(fan(t)):
                    exchange(stream, t, e, h).wait_send()

            @pl.when(jnp.logical_not(collects[stream]))
            def _():
                to_collector(stream, h).wait_send()
        for wrap in range(wraps):
            @pl.when(collector & (level != wrap))
            def _():
                onward(wrap, h).wait_send()


def reduce_and_place(n, groups, kin, total_images, rolled, col_counts):
    slots, gout = rolled.shape
    wraps = kin // slots
    rows = kin // (groups * n)
    blocks = slots // rows
    streams = blocks // groups
    bits = groups.bit_length() - 1
    halves = 2
    dma = pltpu.SemaphoreType.DMA
    fans = [groups >> (t + 1) for t in range(bits)]
    buffers = [pltpu.VMEM((streams, fan, rows, gout), jnp.float32) for fan in fans]
    sems = [dma((streams, fan, halves)) for fan in fans]
    return pl.pallas_call(
        functools.partial(spread, n, groups, wraps, halves, total_images),
        out_shape=jax.ShapeDtypeStruct((rows, gout), jnp.float32),
        in_specs=[
            pl.BlockSpec(memory_space=pltpu.SMEM),
            pl.BlockSpec(memory_space=pltpu.VMEM),
        ],
        out_specs=pl.BlockSpec(memory_space=pltpu.VMEM),
        scratch_shapes=[
            *buffers, *buffers, *sems, *sems,
            pltpu.VMEM((n, rows, gout), jnp.float32),
            pltpu.VMEM((wraps, rows, gout), jnp.float32),
            pltpu.VMEM((rows, gout), jnp.float32),
            dma((streams, halves)), dma((n, halves)), dma((wraps, halves)), dma((halves,)),
        ],
        compiler_params=pltpu.CompilerParams(
            collective_id=1, has_side_effects=True, vmem_limit_bytes=40 * 1024 * 1024),
    )(col_counts, rolled.reshape(blocks, rows, gout))


def shards(patches, grads, basis_g, basis_slots, col_counts):
    groups = lax.axis_size("img")
    owners = lax.axis_size("own")
    kin, slots = basis_slots.shape
    total_images = patches.shape[0] // POS * groups * owners
    corr = partial_corr(owners, patches, grads, basis_g, basis_slots)
    starts = jnp.cumsum(col_counts) - col_counts
    my_start = lax.dynamic_index_in_dim(starts, lax.axis_index("own"), keepdims=False)
    shift = lax.rem(my_start, jnp.int32(slots))
    rolled = lax.dynamic_slice_in_dim(jnp.concatenate([corr, corr], axis=0), slots - shift, slots, 0)
    return reduce_and_place(owners, groups, kin, total_images, rolled, col_counts)


def solution(mesh):
    in_specs = (P(("img", "own"), None), P(("img", "own"), None), P(), P(None, "own"), P())
    out_specs = P(("img", "own"), None)
    return jax.shard_map(shards, mesh=mesh, in_specs=in_specs, out_specs=out_specs, check_vma=False)
```

```python
import functools

import jax
import jax.numpy as jnp
from jax import lax
from jax.experimental import pallas as pl
from jax.experimental.pallas import tpu as pltpu
from jax.sharding import PartitionSpec as P

POS = 49
PIECE = 768
MESH = pl.DeviceIdType.MESH


def widest(total, most):
    return max(w for w in range(128, most + 1, 128) if total % w == 0)


def project(n, images, greet, x_hbm, g_hbm, bg_ref, b_hbm, corr, xbuf, gbuf, bbuf, acc, proj, masked,
            x_sem, g_sem, b_sem, recv, g_recv, right_sem, left_sem, g_right, g_left):
    me = lax.axis_index("own")
    pieces, width, slots = bbuf.shape
    rows = x_hbm.shape[0]
    gout = bg_ref.shape[1]
    tile = widest(slots, 768)
    strip = widest(slots, 256)
    has_left, has_right = me > 0, me < n - 1

    def own_piece(q):
        return pltpu.make_async_copy(
            x_hbm.at[:, pl.ds(pl.multiple_of(q * width, width), width)], xbuf.at[me, q], x_sem.at[q])

    def basis_piece(q):
        return pltpu.make_async_copy(
            b_hbm.at[pl.ds(pl.multiple_of(q * width, width), width)], bbuf.at[q], b_sem.at[q])

    own_g = pltpu.make_async_copy(g_hbm, gbuf.at[me], g_sem)

    def send(chunk, q, to, sem):
        return pltpu.make_async_remote_copy(
            xbuf.at[chunk, q], xbuf.at[chunk, q], sem.at[chunk, q], recv.at[chunk, q],
            device_id={"own": to}, device_id_type=MESH)

    def send_g(chunk, to, sem):
        return pltpu.make_async_remote_copy(
            gbuf.at[chunk], gbuf.at[chunk], sem.at[chunk], g_recv.at[chunk],
            device_id={"own": to}, device_id_type=MESH)

    own_g.start()
    for q in range(pieces):
        own_piece(q).start()
    for q in range(pieces):
        basis_piece(q).start()

    greet()
    own_g.wait()

    @pl.when(has_right)
    def _():
        send_g(me, me + 1, g_right).start()

    @pl.when(has_left)
    def _():
        send_g(me, me - 1, g_left).start()

    def send_own(q, carry):
        own_piece(q).wait()

        @pl.when(has_right)
        def _():
            send(me, q, me + 1, right_sem).start()

        @pl.when(has_left)
        def _():
            send(me, q, me - 1, left_sem).start()
        return carry

    lax.fori_loop(0, pieces, send_own, 0)

    acc[...] = jnp.zeros_like(acc)
    proj[...] = jnp.zeros_like(proj)
    corr[...] = jnp.zeros_like(corr)

    def multiply(chunk, q, side):
        def one(t, carry):
            columns = pl.ds(pl.multiple_of(t * tile, tile), tile)
            acc[side, pl.ds(0, rows), columns] += jnp.dot(
                xbuf[chunk, q], bbuf[q, :, columns], preferred_element_type=jnp.float32)
            return carry
        lax.fori_loop(0, slots // tile, one, 0)

    def finish(chunk, side):
        proj[pl.ds(0, rows), :] = jnp.dot(gbuf[chunk], bg_ref[...], preferred_element_type=jnp.float32)
        whole = proj[...]
        row = lax.broadcasted_iota(jnp.int32, whole.shape, 0)
        for image in range(images):
            inside = (row >= image * POS) & (row < (image + 1) * POS)
            masked[:, image * gout:(image + 1) * gout] = jnp.where(inside, whole, 0.0).astype(jnp.bfloat16)

        def one(t, carry):
            columns = pl.ds(pl.multiple_of(t * strip, strip), strip)
            coef = lax.dot_general(
                acc[side, :, columns].astype(jnp.bfloat16), masked[...], (((0,), (0,)), ((), ())),
                preferred_element_type=jnp.float32)
            for lane in range(gout // 128):
                total = corr[lane, columns, :]
                for image in range(images):
                    part = coef[:, image * gout + lane * 128:image * gout + (lane + 1) * 128]
                    total = total + part * part
                corr[lane, columns, :] = total
            acc[side, :, columns] = jnp.zeros((acc.shape[1], strip), jnp.float32)
            return carry
        lax.fori_loop(0, slots // strip, one, 0)

    def at_distance(d, carry):
        def chunk_of(side):
            return me - d + 2 * d * side

        def present(side):
            chunk = chunk_of(side)
            return (chunk >= 0) & (chunk < n) & ((d > 0) | (side == 0))

        def on_piece(q, carry):
            def on_side(side, carry):
                chunk = chunk_of(side)

                @pl.when(present(side))
                def _():
                    @pl.when(d == 0)
                    def _():
                        basis_piece(q).wait()

                    @pl.when(d > 0)
                    def _():
                        send(chunk, q, me, right_sem).wait_recv()

                        @pl.when((side == 0) & has_right)
                        def _():
                            send(chunk, q, me + 1, right_sem).start()

                        @pl.when((side == 1) & has_left)
                        def _():
                            send(chunk, q, me - 1, left_sem).start()
                    multiply(chunk, q, side)
                return carry
            return lax.fori_loop(0, 2, on_side, carry)
        lax.fori_loop(0, pieces, on_piece, 0)

        def on_end(side, carry):
            chunk = chunk_of(side)

            @pl.when(present(side))
            def _():
                finish(chunk, side)
            return carry

        def on_grads(side, carry):
            chunk = chunk_of(side)

            @pl.when(present(side) & (d > 0))
            def _():
                send_g(chunk, me, g_right).wait_recv()

                @pl.when((side == 0) & has_right)
                def _():
                    send_g(chunk, me + 1, g_right).start()

                @pl.when((side == 1) & has_left)
                def _():
                    send_g(chunk, me - 1, g_left).start()
            return carry
        lax.fori_loop(0, 2, on_grads, 0)
        lax.fori_loop(0, 2, on_end, 0)
        return carry

    lax.fori_loop(0, n, at_distance, 0)

    def drain(chunk, carry):
        @pl.when((chunk <= me) & has_right)
        def _():
            send_g(chunk, me + 1, g_right).wait_send()

        @pl.when((chunk >= me) & has_left)
        def _():
            send_g(chunk, me - 1, g_left).wait_send()

        def one(q, carry):
            @pl.when((chunk <= me) & has_right)
            def _():
                send(chunk, q, me + 1, right_sem).wait_send()

            @pl.when((chunk >= me) & has_left)
            def _():
                send(chunk, q, me - 1, left_sem).wait_send()
            return carry
        lax.fori_loop(0, pieces, one, 0)
        return carry

    return lambda: lax.fori_loop(0, n, drain, 0)


def whole(n, groups, wraps, halves, images, counts, x_hbm, g_hbm, bg_ref, b_hbm, out_ref, corr, x_ref, *scratch):
    ours, scratch = scratch[:15], scratch[15:]
    bits = groups.bit_length() - 1
    recv, sums = scratch[:bits], scratch[bits:2 * bits]
    send_sem, recv_sem = scratch[2 * bits:3 * bits], scratch[3 * bits:4 * bits]
    collected, final, landed, z_send, z_recv, y_send, y_recv = scratch[4 * bits:]
    j, o = lax.axis_index("img"), lax.axis_index("own")
    blocks, rows, gout = x_ref.shape
    part = gout // halves
    run = groups // wraps
    streams = blocks // groups
    level = j // run
    bit = [(j // 2 ** b) % 2 for b in range(bits)]
    orders = [[0] + list(range(1, bits)), [0] + list(range(bits - 1, 0, -1))]

    def partner(b):
        return j + 2 ** b - 2 ** (b + 1) * bit[b]

    def cols(h):
        return pl.ds(h * part, part)

    def greet():
        barrier = pltpu.get_barrier_semaphore()
        greeted = 0
        for b in range(bits):
            pl.semaphore_signal(barrier, inc=1, device_id={"img": partner(b)}, device_id_type=MESH)
            greeted += 1
        for step in range(1, n):
            pl.semaphore_signal(barrier, inc=1, device_id={"own": lax.rem(o + step, n)}, device_id_type=MESH)
            greeted += 1
        for step in range(1, wraps):
            pl.semaphore_signal(barrier, inc=1, device_id={"img": lax.rem(j + step * run, groups)}, device_id_type=MESH)
            greeted += 1
        pl.semaphore_wait(barrier, greeted)

    drain_rows = project(n, images, greet, x_hbm, g_hbm, bg_ref, b_hbm, corr, *ours)

    slots = blocks * rows
    corr[:, pl.ds(slots, rows), :] = corr[:, pl.ds(0, rows), :]
    first, begins, my_start = jnp.int32(0), [], jnp.int32(0)
    for owner in range(n):
        begins.append(first)
        my_start = jnp.where(o == owner, first, my_start)
        first = first + counts[owner]

    def rotate(block):
        base = lax.rem(block * rows + (wraps + 1) * slots - my_start, slots)
        for lane in range(gout // 128):
            x_ref[block, :, lane * 128:(lane + 1) * 128] = corr[lane, pl.ds(base, rows), :]

    def block_of(owner, stream):
        return n * (owner % run) + (owner // run + owner) % wraps + wraps * stream

    def first_block(stream, e, flip):
        owner = 0
        for i, b in enumerate(orders[stream]):
            if i == 0:
                value = 1 - bit[b] if flip else bit[b]
            else:
                value = (e >> (i - 1)) & 1
            owner = owner + value * 2 ** b
        return block_of(owner, stream)

    def source(stream, t, e, flip):
        order = orders[stream]
        if t == 0:
            return x_ref.at[first_block(stream, e, flip)]
        value = 1 - bit[order[t]] if flip else bit[order[t]]
        return sums[t - 1].at[stream, value + 2 * e]

    def exchange(stream, t, e, h):
        return pltpu.make_async_remote_copy(
            source(stream, t, e, True).at[:, cols(h)], recv[t].at[stream, e, :, cols(h)],
            send_sem[t].at[stream, e, h], recv_sem[t].at[stream, e, h],
            device_id={"img": partner(orders[stream][t])}, device_id_type=MESH)

    def fan(t):
        return groups >> (t + 1)

    for stream in range(streams):
        for e in range(fan(0)):
            rotate(first_block(stream, e, True))
    for h in range(halves):
        for stream in range(streams):
            for e in range(fan(0)):
                exchange(stream, 0, e, h).start()
    for stream in range(streams):
        for e in range(fan(0)):
            rotate(first_block(stream, e, False))

    collects = [o == (level + j) % wraps + wraps * stream for stream in range(streams)]
    collector = collects[0]
    for other in collects[1:]:
        collector = collector | other

    def to_collector(stream, h):
        return pltpu.make_async_remote_copy(
            sums[bits - 1].at[stream, 0, :, cols(h)], collected.at[o, :, cols(h)],
            z_send.at[stream, h], z_recv.at[o, h],
            device_id={"own": (level + j) % wraps + wraps * stream}, device_id_type=MESH)

    for t in range(bits):
        for h in range(halves):
            for stream in range(streams):
                for e in range(fan(t)):
                    exchange(stream, t, e, h).wait_recv()
                    sums[t][stream, e, :, cols(h)] = (
                        source(stream, t, e, False)[:, cols(h)] + recv[t][stream, e, :, cols(h)])
                if t + 1 < bits:
                    for e in range(fan(t + 1)):
                        exchange(stream, t + 1, e, h).start()
                else:
                    @pl.when(collects[stream])
                    def _():
                        collected[o, :, cols(h)] = sums[t][stream, 0, :, cols(h)]

                    @pl.when(jnp.logical_not(collects[stream]))
                    def _():
                        to_collector(stream, h).start()

    def onward(wrap, h):
        return pltpu.make_async_remote_copy(
            final.at[wrap, :, cols(h)], landed.at[:, cols(h)], y_send.at[wrap, h], y_recv.at[h],
            device_id={"img": j % run + run * wrap}, device_id_type=MESH)

    for h in range(halves):
        @pl.when(collector)
        def _():
            for step in range(1, n):
                who = lax.rem(o + step, n)
                pltpu.make_async_remote_copy(
                    collected.at[who, :, cols(h)], collected.at[who, :, cols(h)],
                    z_send.at[0, h], z_recv.at[who, h],
                    device_id={"own": who}, device_id_type=MESH).wait_recv()
            for wrap in range(wraps):
                row = (wrap * blocks + n * (j % run) + o) * rows + lax.broadcasted_iota(
                    jnp.int32, (rows, part), 0)
                value = jnp.zeros((rows, part), jnp.float32)
                for owner in range(n):
                    mine = (row >= begins[owner]) & (row < begins[owner] + counts[owner])
                    value = jnp.where(mine, collected[owner, :, cols(h)], value)
                final[wrap, :, cols(h)] = value / jnp.float32(images * groups * n)

                @pl.when(level != wrap)
                def _():
                    onward(wrap, h).start()

                @pl.when(level == wrap)
                def _():
                    out_ref[:, cols(h)] = final[wrap, :, cols(h)]

    from_self = lax.rem(o - j + wraps * (groups + 1), wraps) == level
    for h in range(halves):
        @pl.when(jnp.logical_not(from_self))
        def _():
            onward(0, h).wait_recv()
            out_ref[:, cols(h)] = landed[:, cols(h)]

    for h in range(halves):
        for stream in range(streams):
            for t in range(bits):
                for e in range(fan(t)):
                    exchange(stream, t, e, h).wait_send()

            @pl.when(jnp.logical_not(collects[stream]))
            def _():
                to_collector(stream, h).wait_send()
        for wrap in range(wraps):
            @pl.when(collector & (level != wrap))
            def _():
                onward(wrap, h).wait_send()
    drain_rows()


def shards(patches, grads, basis_g, basis_slots, col_counts):
    groups = lax.axis_size("img")
    n = lax.axis_size("own")
    kin, slots = basis_slots.shape
    gout = basis_g.shape[1]
    patch_rows = patches.shape[0]
    images = patch_rows // POS
    padded = -(-patch_rows // 256) * 256
    width = widest(kin, PIECE)
    pieces = kin // width
    wraps = kin // slots
    rows = kin // (groups * n)
    blocks = slots // rows
    streams = blocks // groups
    bits = groups.bit_length() - 1
    halves = 2
    dma = pltpu.SemaphoreType.DMA
    fans = [groups >> (t + 1) for t in range(bits)]
    buffers = [pltpu.VMEM((streams, fan, rows, gout), jnp.float32) for fan in fans]
    sems = [dma((streams, fan, halves)) for fan in fans]
    return pl.pallas_call(
        functools.partial(whole, n, groups, wraps, halves, images),
        out_shape=jax.ShapeDtypeStruct((rows, gout), jnp.float32),
        in_specs=[
            pl.BlockSpec(memory_space=pltpu.SMEM),
            pl.BlockSpec(memory_space=pl.ANY),
            pl.BlockSpec(memory_space=pl.ANY),
            pl.BlockSpec(memory_space=pltpu.VMEM),
            pl.BlockSpec(memory_space=pl.ANY),
        ],
        out_specs=pl.BlockSpec(memory_space=pltpu.VMEM),
        scratch_shapes=[
            pltpu.VMEM((gout // 128, slots + rows, 128), jnp.float32),
            pltpu.VMEM((blocks, rows, gout), jnp.float32),
            pltpu.VMEM((n, pieces, patch_rows, width), jnp.bfloat16),
            pltpu.VMEM((n, patch_rows, gout), jnp.bfloat16),
            pltpu.VMEM((pieces, width, slots), jnp.bfloat16),
            pltpu.VMEM((2, padded, slots), jnp.float32),
            pltpu.VMEM((padded, gout), jnp.float32),
            pltpu.VMEM((padded, images * gout), jnp.bfloat16),
            dma((pieces,)), dma, dma((pieces,)),
            dma((n, pieces)), dma((n,)), dma((n, pieces)), dma((n, pieces)), dma((n,)), dma((n,)),
            *buffers, *buffers, *sems, *sems,
            pltpu.VMEM((n, rows, gout), jnp.float32),
            pltpu.VMEM((wraps, rows, gout), jnp.float32),
            pltpu.VMEM((rows, gout), jnp.float32),
            dma((streams, halves)), dma((n, halves)), dma((wraps, halves)), dma((halves,)),
        ],
        compiler_params=pltpu.CompilerParams(
            collective_id=0, has_side_effects=True, vmem_limit_bytes=67043328),
    )(col_counts, patches, grads, basis_g, basis_slots)


def solution(mesh):
    in_specs = (P(("img", "own"), None), P(("img", "own"), None), P(), P(None, "own"), P())
    out_specs = P(("img", "own"), None)
    return jax.shard_map(shards, mesh=mesh, in_specs=in_specs, out_specs=out_specs, check_vma=False)
```

```python
import functools

import jax
import jax.numpy as jnp
from jax import lax
from jax.experimental import pallas as pl
from jax.experimental.pallas import tpu as pltpu
from jax.sharding import PartitionSpec as P

POS = 49
PIECE = 768
MESH = pl.DeviceIdType.MESH


def widest(total, most):
    return max(w for w in range(128, most + 1, 128) if total % w == 0)


def project(n, images, greet, x_hbm, g_hbm, bg_ref, b_hbm, corr, xbuf, gbuf, bbuf, acc, proj, masked,
            x_sem, g_sem, b_sem, recv, g_recv, right_sem, left_sem, g_right, g_left):
    me = lax.axis_index("own")
    pieces, width, slots = bbuf.shape
    rows = x_hbm.shape[0]
    gout = bg_ref.shape[1]
    tile = widest(slots, 768)
    strip = widest(slots, 256)
    has_left, has_right = me > 0, me < n - 1

    def own_piece(q):
        return pltpu.make_async_copy(
            x_hbm.at[:, pl.ds(pl.multiple_of(q * width, width), width)], xbuf.at[me, q], x_sem.at[q])

    def basis_piece(q):
        return pltpu.make_async_copy(
            b_hbm.at[pl.ds(pl.multiple_of(q * width, width), width)], bbuf.at[q], b_sem.at[q])

    own_g = pltpu.make_async_copy(g_hbm, gbuf.at[me], g_sem)

    def send(chunk, q, to, sem):
        return pltpu.make_async_remote_copy(
            xbuf.at[chunk, q], xbuf.at[chunk, q], sem.at[chunk, q], recv.at[chunk, q],
            device_id={"own": to}, device_id_type=MESH)

    def send_g(chunk, to, sem):
        return pltpu.make_async_remote_copy(
            gbuf.at[chunk], gbuf.at[chunk], sem.at[chunk], g_recv.at[chunk],
            device_id={"own": to}, device_id_type=MESH)

    own_g.start()
    for q in range(pieces):
        own_piece(q).start()
    for q in range(pieces):
        basis_piece(q).start()

    greet()
    own_g.wait()

    @pl.when(has_right)
    def _():
        send_g(me, me + 1, g_right).start()

    @pl.when(has_left)
    def _():
        send_g(me, me - 1, g_left).start()

    def send_own(q, carry):
        own_piece(q).wait()

        @pl.when(has_right)
        def _():
            send(me, q, me + 1, right_sem).start()

        @pl.when(has_left)
        def _():
            send(me, q, me - 1, left_sem).start()
        return carry

    lax.fori_loop(0, pieces, send_own, 0)

    acc[...] = jnp.zeros_like(acc)
    proj[...] = jnp.zeros_like(proj)
    corr[...] = jnp.zeros_like(corr)

    def multiply(chunk, q, side):
        def one(t, carry):
            columns = pl.ds(pl.multiple_of(t * tile, tile), tile)
            acc[side, pl.ds(0, rows), columns] += jnp.dot(
                xbuf[chunk, q], bbuf[q, :, columns], preferred_element_type=jnp.float32)
            return carry
        lax.fori_loop(0, slots // tile, one, 0)

    def finish(chunk, side):
        proj[pl.ds(0, rows), :] = jnp.dot(gbuf[chunk], bg_ref[...], preferred_element_type=jnp.float32)
        whole = proj[...]
        row = lax.broadcasted_iota(jnp.int32, whole.shape, 0)
        for image in range(images):
            inside = (row >= image * POS) & (row < (image + 1) * POS)
            masked[:, image * gout:(image + 1) * gout] = jnp.where(inside, whole, 0.0).astype(jnp.bfloat16)

        def one(t, carry):
            columns = pl.ds(pl.multiple_of(t * strip, strip), strip)
            coef = lax.dot_general(
                acc[side, :, columns].astype(jnp.bfloat16), masked[...], (((0,), (0,)), ((), ())),
                preferred_element_type=jnp.float32)
            for lane in range(gout // 128):
                total = corr[lane, columns, :]
                for image in range(images):
                    part = coef[:, image * gout + lane * 128:image * gout + (lane + 1) * 128]
                    total = total + part * part
                corr[lane, columns, :] = total
            acc[side, :, columns] = jnp.zeros((acc.shape[1], strip), jnp.float32)
            return carry
        lax.fori_loop(0, slots // strip, one, 0)

    def at_distance(d, carry):
        def chunk_of(side):
            return me - d + 2 * d * side

        def present(side):
            chunk = chunk_of(side)
            return (chunk >= 0) & (chunk < n) & ((d > 0) | (side == 0))

        def on_piece(q, carry):
            def on_side(side, carry):
                chunk = chunk_of(side)

                @pl.when(present(side))
                def _():
                    @pl.when(d == 0)
                    def _():
                        basis_piece(q).wait()

                    @pl.when(d > 0)
                    def _():
                        send(chunk, q, me, right_sem).wait_recv()

                        @pl.when((side == 0) & has_right)
                        def _():
                            send(chunk, q, me + 1, right_sem).start()

                        @pl.when((side == 1) & has_left)
                        def _():
                            send(chunk, q, me - 1, left_sem).start()
                    multiply(chunk, q, side)
                return carry
            return lax.fori_loop(0, 2, on_side, carry)
        lax.fori_loop(0, pieces, on_piece, 0)

        def on_end(side, carry):
            chunk = chunk_of(side)

            @pl.when(present(side))
            def _():
                finish(chunk, side)
            return carry

        def on_grads(side, carry):
            chunk = chunk_of(side)

            @pl.when(present(side) & (d > 0))
            def _():
                send_g(chunk, me, g_right).wait_recv()

                @pl.when((side == 0) & has_right)
                def _():
                    send_g(chunk, me + 1, g_right).start()

                @pl.when((side == 1) & has_left)
                def _():
                    send_g(chunk, me - 1, g_left).start()
            return carry
        lax.fori_loop(0, 2, on_grads, 0)
        lax.fori_loop(0, 2, on_end, 0)
        return carry

    lax.fori_loop(0, n, at_distance, 0)

    def drain(chunk, carry):
        @pl.when((chunk <= me) & has_right)
        def _():
            send_g(chunk, me + 1, g_right).wait_send()

        @pl.when((chunk >= me) & has_left)
        def _():
            send_g(chunk, me - 1, g_left).wait_send()

        def one(q, carry):
            @pl.when((chunk <= me) & has_right)
            def _():
                send(chunk, q, me + 1, right_sem).wait_send()

            @pl.when((chunk >= me) & has_left)
            def _():
                send(chunk, q, me - 1, left_sem).wait_send()
            return carry
        lax.fori_loop(0, pieces, one, 0)
        return carry

    return lambda: lax.fori_loop(0, n, drain, 0)


def whole(n, groups, wraps, halves, images, counts, x_hbm, g_hbm, bg_ref, b_hbm, out_ref, corr, x_ref, *scratch):
    ours, scratch = scratch[:15], scratch[15:]
    bits = groups.bit_length() - 1
    recv, sums = scratch[:bits], scratch[bits:2 * bits]
    send_sem, recv_sem = scratch[2 * bits:3 * bits], scratch[3 * bits:4 * bits]
    collected, final, landed, z_send, z_recv, y_send, y_recv = scratch[4 * bits:]
    j, o = lax.axis_index("img"), lax.axis_index("own")
    blocks, rows, gout = x_ref.shape
    part = gout // halves
    run = groups // wraps
    streams = blocks // groups
    level = j // run
    bit = [(j // 2 ** b) % 2 for b in range(bits)]
    orders = [[0] + list(range(1, bits)), [0] + list(range(bits - 1, 0, -1))]

    def partner(b):
        return j + 2 ** b - 2 ** (b + 1) * bit[b]

    def cols(h):
        return pl.ds(h * part, part)

    def greet():
        barrier = pltpu.get_barrier_semaphore()
        greeted = 0
        for b in range(bits):
            pl.semaphore_signal(barrier, inc=1, device_id={"img": partner(b)}, device_id_type=MESH)
            greeted += 1
        for step in range(1, n):
            pl.semaphore_signal(barrier, inc=1, device_id={"own": lax.rem(o + step, n)}, device_id_type=MESH)
            greeted += 1
        for step in range(1, wraps):
            pl.semaphore_signal(barrier, inc=1, device_id={"img": lax.rem(j + step * run, groups)}, device_id_type=MESH)
            greeted += 1
        pl.semaphore_wait(barrier, greeted)

    drain_rows = project(n, images, greet, x_hbm, g_hbm, bg_ref, b_hbm, corr, *ours)

    slots = blocks * rows
    corr[:, pl.ds(slots, rows), :] = corr[:, pl.ds(0, rows), :]
    first, begins, my_start = jnp.int32(0), [], jnp.int32(0)
    for owner in range(n):
        begins.append(first)
        my_start = jnp.where(o == owner, first, my_start)
        first = first + counts[owner]

    def rotate(block):
        base = lax.rem(block * rows + (wraps + 1) * slots - my_start, slots)
        for lane in range(gout // 128):
            x_ref[block, :, lane * 128:(lane + 1) * 128] = corr[lane, pl.ds(base, rows), :]

    def block_of(owner, stream):
        return n * (owner % run) + (owner // run + owner) % wraps + wraps * stream

    def first_block(stream, e, flip):
        owner = 0
        for i, b in enumerate(orders[stream]):
            if i == 0:
                value = 1 - bit[b] if flip else bit[b]
            else:
                value = (e >> (i - 1)) & 1
            owner = owner + value * 2 ** b
        return block_of(owner, stream)

    def source(stream, t, e, flip):
        order = orders[stream]
        if t == 0:
            return x_ref.at[first_block(stream, e, flip)]
        value = 1 - bit[order[t]] if flip else bit[order[t]]
        return sums[t - 1].at[stream, value + 2 * e]

    def exchange(stream, t, e, h):
        return pltpu.make_async_remote_copy(
            source(stream, t, e, True).at[:, cols(h)], recv[t].at[stream, e, :, cols(h)],
            send_sem[t].at[stream, e, h], recv_sem[t].at[stream, e, h],
            device_id={"img": partner(orders[stream][t])}, device_id_type=MESH)

    def fan(t):
        return groups >> (t + 1)

    for stream in range(streams):
        for e in range(fan(0)):
            rotate(first_block(stream, e, True))
    for h in range(halves):
        for stream in range(streams):
            for e in range(fan(0)):
                exchange(stream, 0, e, h).start()
    for stream in range(streams):
        for e in range(fan(0)):
            rotate(first_block(stream, e, False))

    collects = [o == (level + j) % wraps + wraps * stream for stream in range(streams)]
    collector = collects[0]
    for other in collects[1:]:
        collector = collector | other

    def to_collector(stream, h):
        return pltpu.make_async_remote_copy(
            sums[bits - 1].at[stream, 0, :, cols(h)], collected.at[o, :, cols(h)],
            z_send.at[stream, h], z_recv.at[o, h],
            device_id={"own": (level + j) % wraps + wraps * stream}, device_id_type=MESH)

    for t in range(bits):
        for h in range(halves):
            for stream in range(streams):
                for e in range(fan(t)):
                    exchange(stream, t, e, h).wait_recv()
                    sums[t][stream, e, :, cols(h)] = (
                        source(stream, t, e, False)[:, cols(h)] + recv[t][stream, e, :, cols(h)])
                if t + 1 < bits:
                    for e in range(fan(t + 1)):
                        exchange(stream, t + 1, e, h).start()
                else:
                    @pl.when(collects[stream])
                    def _():
                        collected[o, :, cols(h)] = sums[t][stream, 0, :, cols(h)]

                    @pl.when(jnp.logical_not(collects[stream]))
                    def _():
                        to_collector(stream, h).start()

    def onward(wrap, h):
        return pltpu.make_async_remote_copy(
            final.at[wrap, :, cols(h)], landed.at[:, cols(h)], y_send.at[wrap, h], y_recv.at[h],
            device_id={"img": j % run + run * wrap}, device_id_type=MESH)

    for h in range(halves):
        @pl.when(collector)
        def _():
            for step in range(1, n):
                who = lax.rem(o + step, n)
                pltpu.make_async_remote_copy(
                    collected.at[who, :, cols(h)], collected.at[who, :, cols(h)],
                    z_send.at[0, h], z_recv.at[who, h],
                    device_id={"own": who}, device_id_type=MESH).wait_recv()
            for wrap in range(wraps):
                row = (wrap * blocks + n * (j % run) + o) * rows + lax.broadcasted_iota(
                    jnp.int32, (rows, part), 0)
                value = jnp.zeros((rows, part), jnp.float32)
                for owner in range(n):
                    mine = (row >= begins[owner]) & (row < begins[owner] + counts[owner])
                    value = jnp.where(mine, collected[owner, :, cols(h)], value)
                final[wrap, :, cols(h)] = value / jnp.float32(images * groups * n)

                @pl.when(level != wrap)
                def _():
                    onward(wrap, h).start()

                @pl.when(level == wrap)
                def _():
                    out_ref[:, cols(h)] = final[wrap, :, cols(h)]

    from_self = lax.rem(o - j + wraps * (groups + 1), wraps) == level
    for h in range(halves):
        @pl.when(jnp.logical_not(from_self))
        def _():
            onward(0, h).wait_recv()
            out_ref[:, cols(h)] = landed[:, cols(h)]

    for h in range(halves):
        for stream in range(streams):
            for t in range(bits):
                for e in range(fan(t)):
                    exchange(stream, t, e, h).wait_send()

            @pl.when(jnp.logical_not(collects[stream]))
            def _():
                to_collector(stream, h).wait_send()
        for wrap in range(wraps):
            @pl.when(collector & (level != wrap))
            def _():
                onward(wrap, h).wait_send()
    drain_rows()


def shards(patches, grads, basis_g, basis_slots, col_counts):
    groups = lax.axis_size("img")
    n = lax.axis_size("own")
    kin, slots = basis_slots.shape
    gout = basis_g.shape[1]
    patch_rows = patches.shape[0]
    images = patch_rows // POS
    padded = -(-patch_rows // 256) * 256
    width = widest(kin, PIECE)
    pieces = kin // width
    wraps = kin // slots
    rows = kin // (groups * n)
    blocks = slots // rows
    streams = blocks // groups
    bits = groups.bit_length() - 1
    halves = 4
    dma = pltpu.SemaphoreType.DMA
    fans = [groups >> (t + 1) for t in range(bits)]
    buffers = [pltpu.VMEM((streams, fan, rows, gout), jnp.float32) for fan in fans]
    sems = [dma((streams, fan, halves)) for fan in fans]
    return pl.pallas_call(
        functools.partial(whole, n, groups, wraps, halves, images),
        out_shape=jax.ShapeDtypeStruct((rows, gout), jnp.float32),
        in_specs=[
            pl.BlockSpec(memory_space=pltpu.SMEM),
            pl.BlockSpec(memory_space=pl.ANY),
            pl.BlockSpec(memory_space=pl.ANY),
            pl.BlockSpec(memory_space=pltpu.VMEM),
            pl.BlockSpec(memory_space=pl.ANY),
        ],
        out_specs=pl.BlockSpec(memory_space=pltpu.VMEM),
        scratch_shapes=[
            pltpu.VMEM((gout // 128, slots + rows, 128), jnp.float32),
            pltpu.VMEM((blocks, rows, gout), jnp.float32),
            pltpu.VMEM((n, pieces, patch_rows, width), jnp.bfloat16),
            pltpu.VMEM((n, patch_rows, gout), jnp.bfloat16),
            pltpu.VMEM((pieces, width, slots), jnp.bfloat16),
            pltpu.VMEM((2, padded, slots), jnp.float32),
            pltpu.VMEM((padded, gout), jnp.float32),
            pltpu.VMEM((padded, images * gout), jnp.bfloat16),
            dma((pieces,)), dma, dma((pieces,)),
            dma((n, pieces)), dma((n,)), dma((n, pieces)), dma((n, pieces)), dma((n,)), dma((n,)),
            *buffers, *buffers, *sems, *sems,
            pltpu.VMEM((n, rows, gout), jnp.float32),
            pltpu.VMEM((wraps, rows, gout), jnp.float32),
            pltpu.VMEM((rows, gout), jnp.float32),
            dma((streams, halves)), dma((n, halves)), dma((wraps, halves)), dma((halves,)),
        ],
        compiler_params=pltpu.CompilerParams(
            collective_id=0, has_side_effects=True, vmem_limit_bytes=67043328),
    )(col_counts, patches, grads, basis_g, basis_slots)


def solution(mesh):
    in_specs = (P(("img", "own"), None), P(("img", "own"), None), P(), P(None, "own"), P())
    out_specs = P(("img", "own"), None)
    return jax.shard_map(shards, mesh=mesh, in_specs=in_specs, out_specs=out_specs, check_vma=False)
```
